32 devices in a mesh: seq: 16 (over z, x, core), head: 2 (over y).
Axes of the slice: x: 2, y: 2, z: 4, core: 2. Of those that a mesh axis runs over, the one named last changes fastest.
Arguments:
- queries: bfloat16 [6144, 32, 128], P(('seq', 'head')), may hold values from -6 to 6
- keys: bfloat16 [6144, 8, 128], P('seq', 'head'), may hold values from -6 to 6
- values: bfloat16 [6144, 8, 128], P('seq', 'head'), may hold values from -1.5 to 1.5
- outputs: bfloat16 [6144, 32, 128], P(('seq', 'head')), may hold values from -1.5 to 1.5
- output_gradient: bfloat16 [6144, 32, 128], P(('seq', 'head')), may hold values from -24 to 24
- lse: float32 [6144, 32], P(('seq', 'head')), may hold values from 5.5 to 7.5
Outputs:
- query_grad: bfloat16 [6144, 32, 128], P(('seq', 'head'))
- key_gradient: bfloat16 [6144, 8, 128], P('seq', 'head')
- value_gradient: bfloat16 [6144, 8, 128], P('seq', 'head')
The draws below stay inside these ranges and needn't reach their ends.
All inputs are finite; a program needn't handle non-finite values.
Results may differ from the reference program's by a relative error of at most 0.0068.
Values may be sent and summed in bfloat16 or wider, within the bound.
No kernel may reach another device: no remote copies, remote signals or barrier semaphores. Data moves between devices by JAX's collectives and lax.ppermute only.
A program may use at most 64 MiB of HBM per device.

```python
import jax
import jax.numpy as jnp
from jax import lax

QUERY_HEADS = 32
KEY_VALUE_HEADS = 8
HEAD_SIZE = 128
TOK_DEV = 384
WINDOW = 768
SEQUENCE_TOKENS = 6144
N_SEQ = 16


def steps_of(stream_key, dims, shards, least, largest):
    factor_of = 1.0
    for dim, shards_of in shards:
        draws = jax.random.uniform(jax.random.fold_in(jax.random.fold_in(stream_key, 6), dim), (shards_of,), jnp.float32, least / len(shards), largest / len(shards))
        factor_of = factor_of * jnp.repeat(jnp.exp(draws), dims[dim] // shards_of).reshape((-1,) + (1,) * (len(dims) - 1 - dim))
    return factor_of


def scatter_about(rng, shape, deviation, bound, pieces=(), held_as=jnp.bfloat16):
    array = jax.random.normal(rng, shape, jnp.float32) * deviation
    if len(pieces) > 0:
        array = steps_of(rng, shape, pieces, -0.22, 0.18) * array
    return jnp.clip(array, min=-bound, max=bound).astype(held_as)


def setup_inputs(seed: int = 0) -> dict:
    splits = jax.random.split(jax.random.key(seed), 7)
    return {
        "queries": scatter_about(splits[0], (SEQUENCE_TOKENS, QUERY_HEADS, HEAD_SIZE), 1.0, 6.0, ((0, 32),)),
        "keys": scatter_about(splits[1], (SEQUENCE_TOKENS, KEY_VALUE_HEADS, HEAD_SIZE), 1.0, 6.0, ((0, 16), (1, 2))),
        "values": scatter_about(splits[2], (SEQUENCE_TOKENS, KEY_VALUE_HEADS, HEAD_SIZE), 0.25, 1.5, ((0, 16), (1, 2))),
        "outputs": scatter_about(splits[3], (SEQUENCE_TOKENS, QUERY_HEADS, HEAD_SIZE), 0.25, 1.5, ((0, 32),)),
        "output_gradient": scatter_about(splits[4], (SEQUENCE_TOKENS, QUERY_HEADS, HEAD_SIZE), 4.0, 24.0, ((0, 32),)),
        "lse": jnp.clip(5.5 + 2.0 * jax.random.uniform(splits[5], (SEQUENCE_TOKENS, QUERY_HEADS), jnp.float32) ** steps_of(splits[5], (SEQUENCE_TOKENS, QUERY_HEADS), ((0, 32),), -0.2, 0.2), 5.5, 7.5),
    }


def block_grads(query_blk, grad_blk, output_blk, lse_blk, key_cat, value_cat, block_id):
    token_length = TOK_DEV
    score_scale = HEAD_SIZE ** -0.5
    row_ids = jnp.arange(token_length, dtype=jnp.int32)[:, None]
    col_ids = jnp.arange(3 * token_length, dtype=jnp.int32)[None, :]
    key_pos = block_id * token_length - 2 * token_length + col_ids
    allowed = (key_pos >= 0) & (col_ids > row_ids) & (col_ids <= row_ids + WINDOW)
    query_f = query_blk.astype(jnp.float32)
    grad_f = grad_blk.astype(jnp.float32)
    key_f = key_cat.astype(jnp.float32)
    value_f = value_cat.astype(jnp.float32)
    row_delta = jnp.sum(grad_f * output_blk.astype(jnp.float32), axis=-1)
    row_delta = jnp.transpose(row_delta, (1, 2, 0))[..., None]
    lse_part = jnp.transpose(lse_blk, (1, 2, 0))[..., None]
    scores = jnp.einsum('tkgd,ckd->kgtc', query_f, key_f) * score_scale
    attn_prob = jnp.where(allowed, jnp.exp(scores - lse_part), 0.0)
    prob_bf = lax.optimization_barrier(attn_prob.astype(jnp.bfloat16))
    value_part = jnp.einsum('kgtc,tkgd->ckd', prob_bf.astype(jnp.float32), grad_f)
    prob_grad = jnp.einsum('tkgd,ckd->kgtc', grad_f, value_f)
    score_bf = lax.optimization_barrier((attn_prob * (prob_grad - row_delta) * score_scale).astype(jnp.bfloat16))
    score_f = score_bf.astype(jnp.float32)
    query_grad = jnp.einsum('kgtc,ckd->tkgd', score_f, key_f).astype(jnp.bfloat16)
    key_part = jnp.einsum('kgtc,tkgd->ckd', score_f, query_f)
    return query_grad.reshape(token_length, QUERY_HEADS, HEAD_SIZE), key_part, value_part


def reference(queries, keys, values, outputs, output_gradient, lse):
    token_length = TOK_DEV
    number_of_blocks = N_SEQ
    query_groups = QUERY_HEADS // KEY_VALUE_HEADS
    query_stack = queries.reshape(number_of_blocks, token_length, KEY_VALUE_HEADS, query_groups, HEAD_SIZE)
    gradient_stack = output_gradient.reshape(number_of_blocks, token_length, KEY_VALUE_HEADS, query_groups, HEAD_SIZE)
    output_stack = outputs.reshape(number_of_blocks, token_length, KEY_VALUE_HEADS, query_groups, HEAD_SIZE)
    logsumexp_stack = lse.reshape(number_of_blocks, token_length, KEY_VALUE_HEADS, query_groups)
    key_padded = jnp.concatenate([jnp.zeros((2 * token_length, KEY_VALUE_HEADS, HEAD_SIZE), keys.dtype), keys], 0)
    value_padded = jnp.concatenate([jnp.zeros((2 * token_length, KEY_VALUE_HEADS, HEAD_SIZE), values.dtype), values], 0)

    def advance(carry, inputs):
        pend_key, pend_value = carry
        block_id, query_blk, grad_blk, output_blk, lse_blk = inputs
        start = (block_id * token_length).astype(jnp.int32)
        key_cat = lax.dynamic_slice_in_dim(key_padded, start, 3 * token_length, 0)
        value_cat = lax.dynamic_slice_in_dim(value_padded, start, 3 * token_length, 0)
        query_grad, key_part, value_part = block_grads(query_blk, grad_blk, output_blk, lse_blk, key_cat, value_cat, block_id)
        done_key = pend_key[0] + key_part[:token_length]
        done_value = pend_value[0] + value_part[:token_length]
        next_key = jnp.stack([pend_key[1] + key_part[token_length:2 * token_length], key_part[2 * token_length:]])
        next_value = jnp.stack([pend_value[1] + value_part[token_length:2 * token_length], value_part[2 * token_length:]])
        return (next_key, next_value), (query_grad, done_key, done_value)

    initial_carry = (jnp.zeros((2, token_length, KEY_VALUE_HEADS, HEAD_SIZE), jnp.float32), jnp.zeros((2, token_length, KEY_VALUE_HEADS, HEAD_SIZE), jnp.float32))
    block_ids = jnp.arange(number_of_blocks, dtype=jnp.int32)
    closing_carry, outputs_stacked = lax.scan(advance, initial_carry, (block_ids, query_stack, gradient_stack, output_stack, logsumexp_stack))
    query_grad = outputs_stacked[0].reshape(number_of_blocks * token_length, QUERY_HEADS, HEAD_SIZE)
    key_gradient = jnp.concatenate([outputs_stacked[1][2:].reshape(-1, KEY_VALUE_HEADS, HEAD_SIZE), closing_carry[0].reshape(-1, KEY_VALUE_HEADS, HEAD_SIZE)], 0)
    value_gradient = jnp.concatenate([outputs_stacked[2][2:].reshape(-1, KEY_VALUE_HEADS, HEAD_SIZE), closing_carry[1].reshape(-1, KEY_VALUE_HEADS, HEAD_SIZE)], 0)
    return query_grad, key_gradient.astype(jnp.bfloat16), value_gradient.astype(jnp.bfloat16)
```

```python
import functools
import math

import jax
import jax.numpy as jnp
from jax import lax
from jax.experimental import pallas as pl
from jax.experimental.pallas import tpu as pltpu
from jax.sharding import PartitionSpec as P

LOG2E = math.log2(math.e)
F32 = jnp.float32
BF16 = jnp.bfloat16


def shifted(shard, axis, by):
    size = lax.axis_size(axis)
    pairs = [(i, i + by) for i in range(size) if 0 <= i + by < size]
    return lax.ppermute(shard, axis, pairs)


def swapped(shard, axis):
    return lax.ppermute(shard, axis, [(0, 1), (1, 0)])


def dot(a, b, dims):
    return lax.dot_general(a, b, (dims, ((), ())), preferred_element_type=F32)


def attn_kernel(half, scale, off_ref, *refs):
    (qa, ga, la, da, qb, gb, lb, db, kf, kn, ko, vf, vn, vo) = refs[:14]
    (dqa, dqb, back, prev, own) = refs[14:19]
    (kcat, vcat, dkacc, dvacc, dqacc) = refs[19:]
    length = 2 * half
    for i, (k, v) in enumerate(((kf, vf), (kn, vn), (ko, vo))):
        kcat[pl.ds(i * length, length), :] = k[0]
        vcat[pl.ds(i * length, length), :] = v[0]
    dkacc[...] = jnp.zeros_like(dkacc)
    dvacc[...] = jnp.zeros_like(dvacc)
    rows = qa.shape[1]
    token = lax.broadcasted_iota(jnp.int32, (1, rows), 1)
    token = lax.rem(token, half)
    key_id = lax.broadcasted_iota(jnp.int32, (half, 1), 0)
    tiles = 5
    for i, (q, g, l, d, dq) in enumerate(((qa, ga, la, da, dqa), (qb, gb, lb, db, dqb))):
        off = pl.multiple_of(off_ref[i], half)
        for j in range(tiles):
            span = pl.ds(pl.multiple_of(off + j * half, half), half)
            key = kcat[span, :]
            value = vcat[span, :]
            x = dot(key, q[0], ((1,), (1,))) * (scale * LOG2E) - l[0]
            p = jnp.exp2(x)
            if j == 0:
                p = jnp.where(key_id > token, p, 0.0)
            if j == tiles - 1:
                p = jnp.where(key_id <= token, p, 0.0)
            dvacc[span, :] += dot(p.astype(BF16), g[0], ((1,), (0,)))
            dp = dot(value, g[0], ((1,), (1,)))
            ds = (p * (dp - d[0]) * scale).astype(BF16)
            dkacc[span, :] += dot(ds, q[0], ((1,), (0,)))
            dq_part = dot(ds, key, ((0,), (0,)))
            if j == 0:
                dqacc[...] = dq_part
            elif j < tiles - 1:
                dqacc[...] += dq_part
            else:
                dq[0] = (dqacc[...] + dq_part).astype(BF16)
    for i, acc in enumerate((dkacc, dvacc)):
        back[i, 0] = acc[pl.ds(0, length), :].astype(BF16)
        prev[i, 0] = acc[pl.ds(length, length), :]
        own[i, 0] = acc[pl.ds(2 * length, length), :]


def attention(offs, own_rows, far_rows, kv, first, groups, scale):
    rows, head_dim = own_rows[0].shape[1:]
    length = kv[0].shape[1]
    half = length // 2
    row_spec = pl.BlockSpec((1, rows, head_dim), lambda g, off: (g, 0, 0))
    stat_spec = pl.BlockSpec((1, 1, rows), lambda g, off: (g, 0, 0))
    kv_spec = pl.BlockSpec((1, length, head_dim), lambda g, off: (g + first, 0, 0))
    kv_out = pl.BlockSpec((2, 1, length, head_dim), lambda g, off: (0, g, 0, 0))
    flops = 2 * 2 * 5 * 5 * groups * rows * half * head_dim
    return pl.pallas_call(
        functools.partial(attn_kernel, half, scale),
        grid_spec=pltpu.PrefetchScalarGridSpec(
            num_scalar_prefetch=1,
            grid=(groups,),
            in_specs=[row_spec, row_spec, stat_spec, stat_spec] * 2 + [kv_spec] * 6,
            out_specs=[row_spec, row_spec, kv_out, kv_out, kv_out],
            scratch_shapes=[
                pltpu.VMEM((3 * length, head_dim), BF16),
                pltpu.VMEM((3 * length, head_dim), BF16),
                pltpu.VMEM((3 * length, head_dim), F32),
                pltpu.VMEM((3 * length, head_dim), F32),
                pltpu.VMEM((rows, head_dim), F32),
            ],
        ),
        out_shape=[
            jax.ShapeDtypeStruct((groups, rows, head_dim), BF16),
            jax.ShapeDtypeStruct((groups, rows, head_dim), BF16),
            jax.ShapeDtypeStruct((2, groups, length, head_dim), BF16),
            jax.ShapeDtypeStruct((2, groups, length, head_dim), F32),
            jax.ShapeDtypeStruct((2, groups, length, head_dim), F32),
        ],
        cost_estimate=pl.CostEstimate(
            flops=flops, bytes_accessed=groups * length * head_dim * 60, transcendentals=0
        ),
        name="attention_backward",
    )(offs, *own_rows, *far_rows, *kv)


def body(chunks, queries, keys, values, outputs, output_gradient, lse):
    tokens, heads_all, head_dim = queries.shape
    length, heads_kv, _ = keys.shape
    side = lax.axis_index("head")
    heads = heads_all // lax.axis_size("head")
    per_kv = heads // heads_kv
    groups = heads_kv // chunks
    heads_chunk = heads // chunks
    rows = per_kv * tokens
    scale = head_dim ** (-0.5)

    def piece(x, whose, i):
        x = lax.dynamic_slice_in_dim(x, whose * heads + i * heads_chunk, heads_chunk, 1)
        return x.transpose(1, 0, 2)

    sent = []
    for i in range(chunks):
        sent.append([swapped(piece(x, 1 - side, i), "head") for x in (queries, output_gradient)])
    keys_t = keys.transpose(1, 0, 2)
    near_key = shifted(keys_t, "seq", 1)
    values_t = values.transpose(1, 0, 2)
    near_value = shifted(values_t, "seq", 1)
    delta = jnp.sum(output_gradient.astype(F32) * outputs.astype(F32), axis=-1)
    stats = jnp.stack([(lse * LOG2E).T, delta.T]).reshape(2, -1, 1, rows)
    stats_own = lax.dynamic_slice_in_dim(stats, side * heads_kv, heads_kv, 1)
    stats_far = swapped(lax.dynamic_slice_in_dim(stats, (1 - side) * heads_kv, heads_kv, 1), "head")
    far_key, far_value = shifted((near_key, near_value), "seq", 1)
    kv = (far_key, near_key, keys_t, far_value, near_value, values_t)
    offs = jnp.stack([side, 1 - side]).astype(jnp.int32) * tokens

    own_list, got_list, dkey_list = [], [], []
    for i in range(chunks):
        pick = slice(i * groups, (i + 1) * groups)
        own_rows = [piece(x, side, i).reshape(groups, rows, head_dim) for x in (queries, output_gradient)]
        far_rows = [x.reshape(groups, rows, head_dim) for x in sent[i]]
        dqa, dqb, back, prev, own = attention(
            offs,
            (*own_rows, stats_own[0, pick], stats_own[1, pick]),
            (*far_rows, stats_far[0, pick], stats_far[1, pick]),
            kv,
            i * groups,
            groups,
            scale,
        )
        got_list.append(swapped(dqb.reshape(heads_chunk, tokens, head_dim).transpose(1, 0, 2), "head"))
        own_list.append(dqa.reshape(heads_chunk, tokens, head_dim).transpose(1, 0, 2))
        held = shifted(back, "seq", -1)
        came = shifted((prev + held.astype(F32)).astype(BF16), "seq", -1)
        dkey_list.append((own + came.astype(F32)).astype(BF16))
    query_grad = jnp.zeros(queries.shape, BF16)
    for i in range(chunks):
        query_grad = lax.dynamic_update_slice_in_dim(query_grad, own_list[i], side * heads + i * heads_chunk, 1)
    for i in range(chunks):
        query_grad = lax.dynamic_update_slice_in_dim(query_grad, got_list[i], (1 - side) * heads + i * heads_chunk, 1)
    kv_grad = jnp.concatenate(dkey_list, 1).transpose(0, 2, 1, 3)
    return query_grad, kv_grad[0], kv_grad[1]


def solution(mesh):
    assert mesh.shape["head"] == 2
    return jax.shard_map(
        functools.partial(body, 2),
        mesh=mesh,
        in_specs=(
            P(("seq", "head"), None, None),
            P("seq", "head", None),
            P("seq", "head", None),
            P(("seq", "head"), None, None),
            P(("seq", "head"), None, None),
            P(("seq", "head"), None),
        ),
        out_specs=(P(("seq", "head"), None, None), P("seq", "head", None), P("seq", "head", None)),
        check_vma=False,
    )
```

```python
import functools
import math

import jax
import jax.numpy as jnp
from jax import lax
from jax.experimental import pallas as pl
from jax.experimental.pallas import tpu as pltpu
from jax.sharding import PartitionSpec as P


LOG2E = math.log2(math.e)
F32 = jnp.float32
BF16 = jnp.bfloat16
ACROSS = ((1,), (1,))
INNER = ((1,), (0,))
DOWN = ((0,), (0,))
VMEM = pl.BlockSpec(memory_space=pltpu.VMEM)
SMEM = pl.BlockSpec(memory_space=pltpu.SMEM)
ANY = pl.BlockSpec(memory_space=pl.ANY)
HBM = pl.BlockSpec(memory_space=pltpu.HBM)


def turned(shard, axis, by):
    size = lax.axis_size(axis)
    return lax.ppermute(shard, axis, [(i, (i + by) % size) for i in range(size)])


def swapped(shard, axis):
    return lax.ppermute(shard, axis, [(i, i ^ 1) for i in range(lax.axis_size(axis))])


def dot(a, b, dims):
    return lax.dot_general(a, b, (dims, ((), ())), preferred_element_type=F32)


def params(mib):
    return pltpu.CompilerParams(vmem_limit_bytes=mib * 2**20)


def untangle(x):
    tokens, heads, dim = x.shape
    x = x.astype(F32).reshape(tokens // 2, 2, heads, dim)
    a, b = x[:, 0], x[:, 1]
    low = lax.broadcasted_iota(jnp.int32, a.shape, 1) < heads // 2
    first = jnp.where(low, a, pltpu.roll(b, heads // 2, axis=1))
    second = jnp.where(low, pltpu.roll(a, heads // 2, axis=1), b)
    return [y.reshape(-1, dim).astype(BF16) for y in (first, second)]


def tangle(first, second, tokens):
    rows, dim = first.shape
    heads = 2 * rows // tokens
    a, b = (y.astype(F32).reshape(tokens // 2, heads, dim) for y in (first, second))
    low = lax.broadcasted_iota(jnp.int32, a.shape, 1) < heads // 2
    even = jnp.where(low, a, pltpu.roll(b, heads // 2, axis=1))
    odd = jnp.where(low, pltpu.roll(a, heads // 2, axis=1), b)
    return jnp.stack([even, odd], 1).reshape(tokens, heads, dim).astype(BF16)


def first_kernel(heads, pair, side_ref, place_ref, q, g, q_out, g_out, sem):
    start = pl.multiple_of((1 - side_ref[0]) * heads, pair)
    parts = sem.shape[1]
    size = q.shape[0] // parts
    copies = []
    for n, (src, out) in enumerate(((q, q_out), (g, g_out))):
        for m in range(parts):
            here = pl.ds(m * size, size)
            view = src.at[here, pl.ds(start, pair), :]
            copies.append(pltpu.make_async_copy(view, out.at[here], sem.at[n, m]))
            copies[-1].start()
    for copy in copies:
        copy.wait()


def first(side, place, queries, gradient, heads, pair):
    tokens, _, dim = queries.shape
    return pl.pallas_call(
        functools.partial(first_kernel, heads, pair),
        in_specs=[SMEM, SMEM, HBM, HBM],
        out_specs=[VMEM] * 2,
        out_shape=[jax.ShapeDtypeStruct((tokens, pair, dim), BF16)] * 2,
        scratch_shapes=[pltpu.SemaphoreType.DMA((2, 4))],
        compiler_params=params(2),
        name="first",
    )(side, place, *(pltpu.with_memory_space_constraint(x, pltpu.HBM) for x in (queries, gradient)))


def rest_kernel(heads, pair, side_ref, q, g, *outs):
    outs = list(outs)
    count = heads // pair
    for i in range(1, count):
        start = pl.multiple_of((1 - side_ref[0]) * heads + i * pair, pair)
        rows = [untangle(src[:, pl.ds(start, pair), :]) for src in (q, g)]
        for j in range(2):
            out = outs.pop(0)
            for n in range(2):
                out[n] = rows[n][j]
    for i in range(count):
        start = pl.multiple_of(side_ref[0] * heads + i * pair, pair)
        for src in (q, g):
            out = outs.pop(0)
            out[0], out[1] = untangle(src[:, pl.ds(start, pair), :])


def rest(side, queries, gradient, heads, pair):
    tokens, _, dim = queries.shape
    count = heads // pair
    sizes = [2] * (2 * (count - 1)) + [2] * (2 * count)
    return pl.pallas_call(
        functools.partial(rest_kernel, heads, pair),
        in_specs=[SMEM, VMEM, VMEM],
        out_specs=[VMEM] * len(sizes),
        out_shape=[jax.ShapeDtypeStruct((n, tokens * pair // 2, dim), BF16) for n in sizes],
        compiler_params=params(4),
        name="rest",
    )(side, queries, gradient)


def split_kernel(k, v, whole, *refs):
    outs, (wide, buf, sem) = refs[:-3], refs[-3:]
    heads, length = whole.shape[1:3]
    groups = heads // len(outs)
    parts = sem.shape[1]
    size = k.shape[0] // parts
    copies = []
    for n, src in enumerate((k, v)):
        for m in range(parts):
            here = pl.ds(m * size, size)
            copies.append(pltpu.make_async_copy(src.at[here], buf.at[n, here], sem.at[n, m]))
            copies[-1].start()
    for n in range(2):
        for m in range(parts):
            copies[n * parts + m].wait()
        wide[...] = buf[n].astype(F32)
        for i in range(heads):
            x = wide[pl.ds(i, length, stride=heads), :].astype(BF16)
            whole[n, i] = x
            outs[i // groups][n, i % groups] = x


def split(keys, values, chunks):
    length, heads, dim = keys.shape
    sizes = [heads] + [heads // chunks] * chunks
    return pl.pallas_call(
        split_kernel,
        in_specs=[HBM, HBM],
        out_specs=[VMEM] * (1 + chunks),
        out_shape=[jax.ShapeDtypeStruct((2, n, length, dim), BF16) for n in sizes],
        scratch_shapes=[
            pltpu.VMEM((length * heads, dim), F32),
            pltpu.VMEM((2, length * heads, dim), BF16),
            pltpu.SemaphoreType.DMA((2, 2)),
        ],
        compiler_params=params(4),
        name="split",
    )(*(pltpu.with_memory_space_constraint(x.reshape(-1, dim), pltpu.HBM) for x in (keys, values)))


def parts_of(x, count):
    terms = []
    for _ in range(count):
        terms.append(x.astype(BF16))
        x = x - terms[-1].astype(F32)
    return terms


def stats_kernel(per, side_ref, g, o, lse, ours, other, rep, both):
    tokens, heads_all, dim = g.shape
    rows = tokens * per
    groups = heads_all // per
    lane = lax.broadcasted_iota(jnp.int32, (1, rows), 1)
    token = lax.broadcasted_iota(jnp.int32, (tokens, 1), 0)
    spread = (token == lane // per).astype(F32).astype(BF16)
    for n, term in enumerate(parts_of(lse[...] * LOG2E, 3)):
        part = dot(term, spread, INNER)
        if n == 0:
            rep[...] = part
        else:
            rep[...] += part
    for m in range(groups):
        line = rep[pl.ds(m * per, 1), :]
        for i in range(1, per):
            line = jnp.where(lane % per == i, rep[pl.ds(m * per + i, 1), :], line)
        both[0, pl.ds(m, 1), :] = line
    block = dim // per
    sub = lax.broadcasted_iota(jnp.int32, (1, 2 * per, dim), 1)
    cell = lax.broadcasted_iota(jnp.int32, (1, 2 * per, dim), 2)
    cell = jnp.where(cell % per == sub % per, cell // per, -1)
    which = lax.broadcasted_iota(jnp.int32, (block, 1, 1), 0)

    def tokens_block(t, carry):
        here = pl.ds(pl.multiple_of(t * block, block), block)
        line = pl.ds(pl.multiple_of(t * dim, dim), dim)
        for m in range(groups // 2):
            pick = pl.ds(2 * per * m, 2 * per)
            x = g[here, pick, :].astype(F32) * o[here, pick, :].astype(F32)
            x = jnp.sum(x, axis=-1, keepdims=True)
            x = jnp.sum(jnp.where(cell == which, x, 0.0), axis=0)
            for n in range(2):
                both[1, pl.ds(2 * m + n, 1), line] = jnp.sum(x[n * per : (n + 1) * per], axis=0, keepdims=True)
        return carry

    lax.fori_loop(0, tokens // block, tokens_block, 0)
    half = groups // 2
    side = side_ref[0]
    for n in range(2):
        low, high = both[n, pl.ds(0, half), :], both[n, pl.ds(half, half), :]
        ours[n] = jnp.where(side == 0, low, high)
        other[n] = jnp.where(side == 0, high, low)


def row_stats(side, gradient, outputs, lse, per):
    tokens, heads_all, _ = gradient.shape
    groups, rows = heads_all // per, tokens * per
    return pl.pallas_call(
        functools.partial(stats_kernel, per),
        in_specs=[SMEM, VMEM, VMEM, VMEM],
        out_specs=[VMEM, VMEM],
        out_shape=[jax.ShapeDtypeStruct((2, groups // 2, rows), F32)] * 2,
        scratch_shapes=[pltpu.VMEM((heads_all, rows), F32), pltpu.VMEM((2, groups, rows), F32)],
        compiler_params=params(8),
        name="row_stats",
    )(side, gradient, outputs, lse.T)


def join_kernel(where, blocks, place_ref, *refs):
    groups = len(where)
    here, came = refs[:groups], refs[groups:-3]
    outs, wide = refs[-3:-1], refs[-1]
    prev, back = came[: len(came) // 2], came[len(came) // 2 :]
    length = wide.shape[0] // groups
    even = place_ref[0] % 2 == 0
    inside = place_ref[0] < blocks - 2
    for n, out in enumerate(outs):
        for i, (m, at) in enumerate(where):
            total = here[i][n, pl.ds(2 * length, length), :]
            total += jnp.where(even, prev[m][n, at].astype(F32), 0.0)
            total += jnp.where(inside, back[m][n, at].astype(F32), 0.0)
            wide[pl.ds(i, length, stride=groups), :] = total
        out[...] = wide[...].astype(BF16)


def join(place, blocks, here, prev, back):
    groups = len(here)
    where = tuple((m, at) for m, x in enumerate(prev) for at in range(x.shape[1]))
    length, dim = prev[0].shape[2:]
    shape = (length * groups, dim)
    outs = pl.pallas_call(
        functools.partial(join_kernel, where, blocks),
        in_specs=[SMEM] + [VMEM] * (groups + 2 * len(prev)),
        out_specs=[VMEM] * 2,
        out_shape=[jax.ShapeDtypeStruct(shape, BF16)] * 2,
        scratch_shapes=[pltpu.VMEM(shape, F32)],
        compiler_params=params(4),
        name="join",
    )(place, *here, *prev, *back)
    return [x.reshape(length, groups, dim) for x in outs]


def merge_kernel(place_ref, *refs):
    here, prev, out = refs[:-2], refs[-2], refs[-1]
    length = prev.shape[2]
    odd = place_ref[0] % 2 == 1
    for n in range(2):
        for i, acc in enumerate(here):
            out[n, i] = (acc[n, pl.ds(0, length), :] + jnp.where(odd, prev[n, i].astype(F32), 0.0)).astype(BF16)


def merge(place, here, prev):
    return pl.pallas_call(
        merge_kernel,
        in_specs=[SMEM] + [VMEM] * (len(here) + 1),
        out_specs=VMEM,
        out_shape=jax.ShapeDtypeStruct(prev.shape, BF16),
        compiler_params=params(2),
        name="merge",
    )(place, *here, prev)


def place_kernel(plan, heads, side_ref, *refs):
    buf, sem = refs[-2:]
    out = refs[-3]
    tokens, pair = buf.shape[1:3]
    copies = []
    for m, (a, b, ours, first) in enumerate(plan):
        side = side_ref[0] if ours else 1 - side_ref[0]
        start = pl.multiple_of(side * heads + first, pair)
        buf[m] = tangle(refs[a[0]][a[1]], refs[b[0]][b[1]], tokens)
        copies.append(pltpu.make_async_copy(buf.at[m], out.at[:, pl.ds(start, pair), :], sem.at[m]))
        copies[-1].start()
    for copy in copies:
        copy.wait()


def place(side, pieces, plan, whole, shape, heads, pair):
    more = [] if whole is None else [whole]
    return pl.pallas_call(
        functools.partial(place_kernel, plan, heads),
        in_specs=[SMEM] + [VMEM] * len(pieces) + [ANY] * len(more),
        out_specs=ANY,
        out_shape=jax.ShapeDtypeStruct(shape, BF16),
        scratch_shapes=[
            pltpu.VMEM((len(plan), shape[0], pair, shape[2]), BF16),
            pltpu.SemaphoreType.DMA((len(plan),)),
        ],
        input_output_aliases={1 + len(pieces): 0} if more else {},
        compiler_params=params(4),
        name="place",
    )(side, *pieces, *more)


def attn_kernel(scale, spots, ours, add, side_ref, place_ref, q, g, stats, far, far_next, own_next, own, *refs):
    groups = len(spots)
    refs = list(refs[groups:] if add else refs)
    dq = refs.pop(0)
    accs = [refs.pop(0) for _ in range(groups)]
    kcat, vcat, qs, gs = refs[-4:]
    length = own.shape[2]
    rows, dim = dq.shape[1:]
    behind = 0 if ours else 1
    if q.shape[1] != rows:
        behind = 0
        for src, dst in ((q, qs), (g, gs)):
            dst[0], dst[1] = untangle(src[...])
        q, g = qs, gs
    place = place_ref[0]

    def fill(block, src, index, when):
        here = pl.ds(block * length, length)

        @pl.when(when)
        def _():
            for i, spot in enumerate(spots):
                kcat[i, here, :] = jnp.zeros((length, dim), BF16) if src is None else src[0, spot[index]]
                vcat[i, here, :] = jnp.zeros((length, dim), BF16) if src is None else src[1, spot[index]]

    fill(0, far, 2, place >= 2)
    fill(0, None, 2, place < 2)
    fill(1, own_next, 1, place % 2 == 1)
    fill(1, far_next, 2, jnp.logical_and(place % 2 == 0, place >= 2))
    fill(1, None, 2, place < 1)
    fill(2, own, 1, place >= 0)
    if not add:
        for acc in accs:
            acc[...] = jnp.zeros_like(acc)

    width = 256
    half = length // 2
    per = rows // half
    span = width // per
    window = 2 * length
    token = lax.broadcasted_iota(jnp.int32, (1, width), 1) // per
    key_id = lax.broadcasted_iota(jnp.int32, (span, 1), 0)
    side = side_ref[0] if ours else 1 - side_ref[0]
    off = pl.multiple_of(side * half, span)

    def operands(i, b):
        here = pl.ds(b * width, width)
        keys = pl.ds(pl.multiple_of(off + b * span, span), window + span)
        return q[spots[i][0], here, :], g[spots[i][0] + behind, here, :], keys, here

    def scores(i, b):
        qb, gb, keys, _ = operands(i, b)
        return dot(kcat[i, keys, :], qb, ACROSS), dot(vcat[i, keys, :], gb, ACROSS)

    def weights(i, b, s, dp):
        here = pl.ds(b * width, width)
        at = pl.ds(spots[i][1], 1)
        p = jnp.exp2(s * (scale * LOG2E) - stats[0, at, here])
        first = jnp.where(key_id > token, p[:span], 0.0)
        last = jnp.where(key_id <= token, p[window:], 0.0)
        p = jnp.concatenate([first, p[span:window], last], 0)
        ds = p * (dp - stats[1, at, here]) * scale
        return p.astype(BF16), ds.astype(BF16)

    steps = [(i, b) for i in range(groups) for b in range(rows // width)]
    ahead = scores(*steps[0])
    for m, (i, b) in enumerate(steps):
        now = ahead
        if m + 1 < len(steps):
            ahead = scores(*steps[m + 1])
        p, ds = weights(i, b, *now)
        qb, gb, keys, here = operands(i, b)
        accs[i][1, keys, :] += dot(p, gb, INNER)
        accs[i][0, keys, :] += dot(ds, qb, INNER)
        dq[i, here, :] = dot(ds, kcat[i, keys, :], DOWN).astype(BF16)
    if add:
        prev = refs[0]
        for n in range(2):
            for i in range(groups):
                prev[n, i] = accs[i][n, pl.ds(length, length), :].astype(BF16)


def attention(side, place, q, g, stats, kv, accs, spots, ours, scale):
    length, dim = kv[0].shape[2:]
    rows = stats.shape[2]
    groups = len(spots)
    add = accs is not None
    out_shape = [jax.ShapeDtypeStruct((groups, rows, dim), BF16)]
    out_shape += [jax.ShapeDtypeStruct((2, 3 * length, dim), F32)] * groups
    if add:
        out_shape += [jax.ShapeDtypeStruct((2, groups, length, dim), BF16)]
    operands = [q, g, stats, *kv] + list(accs or ())
    flops = 2 * 5 * groups * rows * (2 * length + 64) * dim
    return pl.pallas_call(
        functools.partial(attn_kernel, scale, spots, ours, add),
        in_specs=[SMEM, SMEM] + [VMEM] * len(operands),
        out_specs=[VMEM] * len(out_shape),
        out_shape=out_shape,
        scratch_shapes=[pltpu.VMEM((groups, 3 * length, dim), BF16)] * 2 + [pltpu.VMEM((2, rows, dim), BF16)] * 2,
        input_output_aliases={9 + i: 1 + i for i in range(groups)} if add else {},
        compiler_params=params(16),
        cost_estimate=pl.CostEstimate(flops=flops, bytes_accessed=0, transcendentals=0),
        name="attention",
    )(side, place, *operands)


def body(queries, keys, values, outputs, output_gradient, lse):
    _, heads_all, dim = queries.shape
    _, heads_kv, _ = keys.shape
    side = lax.axis_index("head")
    heads = heads_all // lax.axis_size("head")
    per = heads // heads_kv
    chunks = heads_kv // 2
    pair = 2 * per
    scale = dim ** (-0.5)
    side_s = side.astype(jnp.int32).reshape(1)
    place_s = lax.axis_index("seq").astype(jnp.int32).reshape(1)

    packed = first(side_s, place_s, queries, output_gradient, heads, pair)
    own_kv, *chunk_kv = split(keys, values, chunks)
    far_kv, far_next = [], []
    for i in range(chunks):
        far_kv.append(turned(chunk_kv[i], "seq", 2))
        far_next.append(swapped(far_kv[i], "seq"))
    own_next = swapped(own_kv, "seq")
    stats, stats_other = row_stats(side_s, output_gradient, outputs, lse, per)
    stats_got = swapped(stats_other, "head")
    others = rest(side_s, queries, output_gradient, heads, pair)
    mine_rows = others[2 * (chunks - 1) :]
    got = []
    got.append([swapped(packed[0], "head")])
    got[0].append(swapped(packed[1], "head"))
    for i, two in enumerate(others[: 2 * (chunks - 1)]):
        got.append([swapped(two, "head")] * 2)

    run = functools.partial(attention, side_s, place_s, scale=scale)
    ours, theirs, accs, prev_got, back_got = [], [], [], [], []
    count = 0
    for i in range(chunks):
        kv = (far_kv[i], far_next[i], own_next, own_kv)
        spots = tuple((j, 2 * i + j, j) for j in range(2))
        dq, *acc = run(*mine_rows[2 * i : 2 * i + 2], stats, kv, None, spots, True)
        ours.append(dq)
        for task in ((0, 1),) if i == 0 else ((0,), (1,)):
            spots = tuple((j if i == 0 else 0, 2 * i + j, j) for j in task)
            dq, *out, prev = run(*got[count], stats_got, kv, [acc[j] for j in task], spots, False)
            accs += out
            prev_got.append(swapped(prev, "seq"))
            theirs.append(swapped(dq, "head"))
            back_got.append(turned(merge(place_s, out, prev_got[-1]), "seq", -2))
            count += 1
    plan = [((i, 0), (i, 1), True, i * pair) for i in range(chunks)]
    plan += [((chunks, 0), (chunks, 1), False, 0)]
    plan += [((chunks + 2 * i - 1, 0), (chunks + 2 * i, 0), False, i * pair) for i in range(1, chunks - 1)]
    whole = place(side_s, ours + theirs[:-2], tuple(plan), None, queries.shape, heads, pair)
    plan = (((0, 0), (1, 0), False, (chunks - 1) * pair),)
    whole = place(side_s, theirs[-2:], plan, whole, queries.shape, heads, pair)
    return whole, *join(place_s, lax.axis_size("seq"), accs, prev_got, back_got)


def solution(mesh):
    assert mesh.shape["head"] == 2

    return jax.shard_map(
        body,
        mesh=mesh,
        in_specs=(
            P(("seq", "head"), None, None),
            P("seq", "head", None),
            P("seq", "head", None),
            P(("seq", "head"), None, None),
            P(("seq", "head"), None, None),
            P(("seq", "head"), None),
        ),
        out_specs=(P(("seq", "head"), None, None), P("seq", "head", None), P("seq", "head", None)),
        check_vma=False,
    )
```

```python
import functools
import math

import jax
import jax.numpy as jnp
from jax import lax
from jax.experimental import pallas as pl
from jax.experimental.pallas import tpu as pltpu
from jax.sharding import PartitionSpec as P


LOG2E = math.log2(math.e)
F32 = jnp.float32
BF16 = jnp.bfloat16
ACROSS = ((1,), (1,))
INNER = ((1,), (0,))
DOWN = ((0,), (0,))
VMEM = pl.BlockSpec(memory_space=pltpu.VMEM)
SMEM = pl.BlockSpec(memory_space=pltpu.SMEM)
ANY = pl.BlockSpec(memory_space=pl.ANY)
HBM = pl.BlockSpec(memory_space=pltpu.HBM)


def turned(shard, axis, by):
    size = lax.axis_size(axis)
    return lax.ppermute(shard, axis, [(i, (i + by) % size) for i in range(size)])


def swapped(shard, axis):
    return lax.ppermute(shard, axis, [(i, i ^ 1) for i in range(lax.axis_size(axis))])


def dot(a, b, dims):
    return lax.dot_general(a, b, (dims, ((), ())), preferred_element_type=F32)


def params(mib):
    return pltpu.CompilerParams(vmem_limit_bytes=mib * 2**20)


def untangle(x):
    tokens, heads, dim = x.shape
    x = x.astype(F32).reshape(tokens // 2, 2, heads, dim)
    a, b = x[:, 0], x[:, 1]
    low = lax.broadcasted_iota(jnp.int32, a.shape, 1) < heads // 2
    first = jnp.where(low, a, pltpu.roll(b, heads // 2, axis=1))
    second = jnp.where(low, pltpu.roll(a, heads // 2, axis=1), b)
    return [y.reshape(-1, dim).astype(BF16) for y in (first, second)]


def tangle(first, second, tokens):
    rows, dim = first.shape
    heads = 2 * rows // tokens
    a, b = (y.astype(F32).reshape(tokens // 2, heads, dim) for y in (first, second))
    low = lax.broadcasted_iota(jnp.int32, a.shape, 1) < heads // 2
    even = jnp.where(low, a, pltpu.roll(b, heads // 2, axis=1))
    odd = jnp.where(low, pltpu.roll(a, heads // 2, axis=1), b)
    return jnp.stack([even, odd], 1).reshape(tokens, heads, dim).astype(BF16)


def first_kernel(heads, pair, side_ref, place_ref, src, out, sem):
    start = pl.multiple_of((1 - side_ref[0]) * heads, pair)
    parts = sem.shape[0]
    size = src.shape[0] // parts
    copies = []
    for m in range(parts):
        here = pl.ds(m * size, size)
        copies.append(pltpu.make_async_copy(src.at[here, pl.ds(start, pair), :], out.at[here], sem.at[m]))
        copies[-1].start()
    for copy in copies:
        copy.wait()


def first(side, place, x, heads, pair):
    tokens, _, dim = x.shape
    return pl.pallas_call(
        functools.partial(first_kernel, heads, pair),
        in_specs=[SMEM, SMEM, HBM],
        out_specs=VMEM,
        out_shape=jax.ShapeDtypeStruct((tokens, pair, dim), BF16),
        scratch_shapes=[pltpu.SemaphoreType.DMA((4,))],
        compiler_params=params(2),
        name="first",
    )(side, place, pltpu.with_memory_space_constraint(x, pltpu.HBM))


def rest_kernel(heads, pair, side_ref, q, g, *outs):
    outs = list(outs)
    count = heads // pair
    for i in range(1, count):
        start = pl.multiple_of((1 - side_ref[0]) * heads + i * pair, pair)
        rows = [untangle(src[:, pl.ds(start, pair), :]) for src in (q, g)]
        for j in range(2):
            out = outs.pop(0)
            for n in range(2):
                out[n] = rows[n][j]
    for i in range(count):
        start = pl.multiple_of(side_ref[0] * heads + i * pair, pair)
        for src in (q, g):
            out = outs.pop(0)
            out[0], out[1] = untangle(src[:, pl.ds(start, pair), :])


def rest(side, queries, gradient, heads, pair):
    tokens, _, dim = queries.shape
    count = heads // pair
    sizes = [2] * (2 * (count - 1)) + [2] * (2 * count)
    return pl.pallas_call(
        functools.partial(rest_kernel, heads, pair),
        in_specs=[SMEM, VMEM, VMEM],
        out_specs=[VMEM] * len(sizes),
        out_shape=[jax.ShapeDtypeStruct((n, tokens * pair // 2, dim), BF16) for n in sizes],
        compiler_params=params(4),
        name="rest",
    )(side, queries, gradient)


def split_kernel(k, v, whole, *refs):
    outs, (wide, buf, sem) = refs[:-3], refs[-3:]
    heads, length = whole.shape[1:3]
    groups = heads // len(outs)
    parts = sem.shape[1]
    size = k.shape[0] // parts
    copies = []
    for n, src in enumerate((k, v)):
        for m in range(parts):
            here = pl.ds(m * size, size)
            copies.append(pltpu.make_async_copy(src.at[here], buf.at[n, here], sem.at[n, m]))
            copies[-1].start()
    for n in range(2):
        for m in range(parts):
            copies[n * parts + m].wait()
        wide[...] = buf[n].astype(F32)
        for i in range(heads):
            x = wide[pl.ds(i, length, stride=heads), :].astype(BF16)
            whole[n, i] = x
            outs[i // groups][n, i % groups] = x


def split(keys, values, chunks):
    length, heads, dim = keys.shape
    sizes = [heads] + [heads // chunks] * chunks
    return pl.pallas_call(
        split_kernel,
        in_specs=[HBM, HBM],
        out_specs=[VMEM] * (1 + chunks),
        out_shape=[jax.ShapeDtypeStruct((2, n, length, dim), BF16) for n in sizes],
        scratch_shapes=[
            pltpu.VMEM((length * heads, dim), F32),
            pltpu.VMEM((2, length * heads, dim), BF16),
            pltpu.SemaphoreType.DMA((2, 2)),
        ],
        compiler_params=params(4),
        name="split",
    )(*(pltpu.with_memory_space_constraint(x.reshape(-1, dim), pltpu.HBM) for x in (keys, values)))


def parts_of(x, count):
    terms = []
    for _ in range(count):
        terms.append(x.astype(BF16))
        x = x - terms[-1].astype(F32)
    return terms


def stats_kernel(per, side_ref, g, o, lse, ours, other, rep, both):
    tokens, heads_all, dim = g.shape
    rows = tokens * per
    groups = heads_all // per
    lane = lax.broadcasted_iota(jnp.int32, (1, rows), 1)
    token = lax.broadcasted_iota(jnp.int32, (tokens, 1), 0)
    spread = (token == lane // per).astype(F32).astype(BF16)
    for n, term in enumerate(parts_of(lse[...] * LOG2E, 3)):
        part = dot(term, spread, INNER)
        if n == 0:
            rep[...] = part
        else:
            rep[...] += part
    for m in range(groups):
        line = rep[pl.ds(m * per, 1), :]
        for i in range(1, per):
            line = jnp.where(lane % per == i, rep[pl.ds(m * per + i, 1), :], line)
        both[0, pl.ds(m, 1), :] = line
    block = dim // per
    sub = lax.broadcasted_iota(jnp.int32, (1, 2 * per, dim), 1)
    cell = lax.broadcasted_iota(jnp.int32, (1, 2 * per, dim), 2)
    cell = jnp.where(cell % per == sub % per, cell // per, -1)
    which = lax.broadcasted_iota(jnp.int32, (block, 1, 1), 0)

    def tokens_block(t, carry):
        here = pl.ds(pl.multiple_of(t * block, block), block)
        line = pl.ds(pl.multiple_of(t * dim, dim), dim)
        for m in range(groups // 2):
            pick = pl.ds(2 * per * m, 2 * per)
            x = g[here, pick, :].astype(F32) * o[here, pick, :].astype(F32)
            x = jnp.sum(x, axis=-1, keepdims=True)
            x = jnp.sum(jnp.where(cell == which, x, 0.0), axis=0)
            for n in range(2):
                both[1, pl.ds(2 * m + n, 1), line] = jnp.sum(x[n * per : (n + 1) * per], axis=0, keepdims=True)
        return carry

    lax.fori_loop(0, tokens // block, tokens_block, 0)
    half = groups // 2
    side = side_ref[0]
    for n in range(2):
        low, high = both[n, pl.ds(0, half), :], both[n, pl.ds(half, half), :]
        ours[n] = jnp.where(side == 0, low, high)
        other[n] = jnp.where(side == 0, high, low)


def row_stats(side, gradient, outputs, lse, per):
    tokens, heads_all, _ = gradient.shape
    groups, rows = heads_all // per, tokens * per
    return pl.pallas_call(
        functools.partial(stats_kernel, per),
        in_specs=[SMEM, VMEM, VMEM, VMEM],
        out_specs=[VMEM, VMEM],
        out_shape=[jax.ShapeDtypeStruct((2, groups // 2, rows), F32)] * 2,
        scratch_shapes=[pltpu.VMEM((heads_all, rows), F32), pltpu.VMEM((2, groups, rows), F32)],
        compiler_params=params(8),
        name="row_stats",
    )(side, gradient, outputs, lse.T)


def gather_kernel(where, blocks, place_ref, *refs):
    groups = len(where)
    here, came, outs = refs[:groups], refs[groups:-2], refs[-2:]
    prev, back = came[: len(came) // 2 + 1], came[len(came) // 2 + 1 :]
    length = outs[0].shape[0] // groups
    even = place_ref[0] % 2 == 0
    inside = place_ref[0] < blocks - 2
    for n, out in enumerate(outs):
        for i, (m, at) in enumerate(where):
            total = here[i][n, pl.ds(2 * length, length), :]
            total += jnp.where(even, prev[m][n, at].astype(F32), 0.0)
            if m < len(back):
                total += jnp.where(inside, back[m][n, at].astype(F32), 0.0)
            out[pl.ds(i, length, stride=groups), :] = total


def gather(place, blocks, here, prev, back):
    groups = len(here)
    where = tuple((m, at) for m, x in enumerate(prev) for at in range(x.shape[1]))
    length, dim = prev[0].shape[2:]
    return pl.pallas_call(
        functools.partial(gather_kernel, where, blocks),
        in_specs=[SMEM] + [VMEM] * (groups + len(prev) + len(back)),
        out_specs=[VMEM] * 2,
        out_shape=[jax.ShapeDtypeStruct((length * groups, dim), F32)] * 2,
        compiler_params=params(2),
        name="gather",
    )(place, *here, *prev, *back)


def join_kernel(blocks, place_ref, last, wide_k, wide_v, out_k, out_v, sum_k, sum_v):
    length = last.shape[2]
    groups = wide_k.shape[0] // length
    inside = place_ref[0] < blocks - 2
    for n, (out, total) in enumerate(((out_k, sum_k), (out_v, sum_v))):
        rows = pl.ds(groups - 1, length, stride=groups)
        total[rows, :] = total[rows, :] + jnp.where(inside, last[n, 0].astype(F32), 0.0)
        out[...] = total[...].astype(BF16)


def join(place, blocks, last, wide):
    shape = wide[0].shape
    length, dim = last.shape[2:]
    outs = pl.pallas_call(
        functools.partial(join_kernel, blocks),
        in_specs=[SMEM] + [VMEM] * 3,
        out_specs=[VMEM] * 4,
        out_shape=[jax.ShapeDtypeStruct(shape, t) for t in (BF16, BF16, F32, F32)],
        input_output_aliases={2: 2, 3: 3},
        compiler_params=params(2),
        name="join",
    )(place, last, *wide)
    return [x.reshape(length, shape[0] // length, dim) for x in outs[:2]]


def merge_kernel(place_ref, *refs):
    here, prev, out = refs[:-2], refs[-2], refs[-1]
    length = prev.shape[2]
    odd = place_ref[0] % 2 == 1
    for n in range(2):
        for i, acc in enumerate(here):
            out[n, i] = (acc[n, pl.ds(0, length), :] + jnp.where(odd, prev[n, i].astype(F32), 0.0)).astype(BF16)


def merge(place, here, prev):
    return pl.pallas_call(
        merge_kernel,
        in_specs=[SMEM] + [VMEM] * (len(here) + 1),
        out_specs=VMEM,
        out_shape=jax.ShapeDtypeStruct(prev.shape, BF16),
        compiler_params=params(2),
        name="merge",
    )(place, *here, prev)


def place_kernel(plan, heads, side_ref, *refs):
    buf, sem = refs[-2:]
    out = refs[-3]
    tokens, pair = buf.shape[1:3]
    copies = []
    for m, (a, b, ours, first) in enumerate(plan):
        side = side_ref[0] if ours else 1 - side_ref[0]
        start = pl.multiple_of(side * heads + first, pair)
        buf[m] = tangle(refs[a[0]][a[1]], refs[b[0]][b[1]], tokens)
        copies.append(pltpu.make_async_copy(buf.at[m], out.at[:, pl.ds(start, pair), :], sem.at[m]))
        copies[-1].start()
    for copy in copies:
        copy.wait()


def place(side, pieces, plan, whole, shape, heads, pair):
    more = [] if whole is None else [whole]
    return pl.pallas_call(
        functools.partial(place_kernel, plan, heads),
        in_specs=[SMEM] + [VMEM] * len(pieces) + [ANY] * len(more),
        out_specs=ANY,
        out_shape=jax.ShapeDtypeStruct(shape, BF16),
        scratch_shapes=[
            pltpu.VMEM((len(plan), shape[0], pair, shape[2]), BF16),
            pltpu.SemaphoreType.DMA((len(plan),)),
        ],
        input_output_aliases={1 + len(pieces): 0} if more else {},
        compiler_params=params(4),
        name="place",
    )(side, *pieces, *more)


def attn_kernel(scale, spots, ours, add, side_ref, place_ref, q, g, stats, far, far_next, own_next, own, *refs):
    groups = len(spots)
    refs = list(refs[groups:] if add else refs)
    dq = refs.pop(0)
    accs = [refs.pop(0) for _ in range(groups)]
    kcat, vcat, qs, gs = refs[-4:]
    length = own.shape[2]
    rows, dim = dq.shape[1:]
    behind = 0 if ours else 1
    if q.shape[1] != rows:
        behind = 0
        for src, dst in ((q, qs), (g, gs)):
            dst[0], dst[1] = untangle(src[...])
        q, g = qs, gs
    place = place_ref[0]

    def fill(block, src, index, when):
        here = pl.ds(block * length, length)

        @pl.when(when)
        def _():
            for i, spot in enumerate(spots):
                kcat[i, here, :] = jnp.zeros((length, dim), BF16) if src is None else src[0, spot[index]]
                vcat[i, here, :] = jnp.zeros((length, dim), BF16) if src is None else src[1, spot[index]]

    fill(0, far, 2, place >= 2)
    fill(0, None, 2, place < 2)
    fill(1, own_next, 1, place % 2 == 1)
    fill(1, far_next, 2, jnp.logical_and(place % 2 == 0, place >= 2))
    fill(1, None, 2, place < 1)
    fill(2, own, 1, place >= 0)
    if not add:
        for acc in accs:
            acc[...] = jnp.zeros_like(acc)

    width = 256
    half = length // 2
    per = rows // half
    span = width // per
    window = 2 * length
    token = lax.broadcasted_iota(jnp.int32, (1, width), 1) // per
    key_id = lax.broadcasted_iota(jnp.int32, (span, 1), 0)
    side = side_ref[0] if ours else 1 - side_ref[0]
    off = pl.multiple_of(side * half, span)

    def operands(i, b):
        here = pl.ds(b * width, width)
        keys = pl.ds(pl.multiple_of(off + b * span, span), window + span)
        return q[spots[i][0], here, :], g[spots[i][0] + behind, here, :], keys, here

    def scores(i, b):
        qb, gb, keys, _ = operands(i, b)
        return dot(kcat[i, keys, :], qb, ACROSS), dot(vcat[i, keys, :], gb, ACROSS)

    def weights(i, b, s, dp):
        here = pl.ds(b * width, width)
        at = pl.ds(spots[i][1], 1)
        p = jnp.exp2(s * (scale * LOG2E) - stats[0, at, here])
        first = jnp.where(key_id > token, p[:span], 0.0)
        last = jnp.where(key_id <= token, p[window:], 0.0)
        p = jnp.concatenate([first, p[span:window], last], 0)
        ds = p * (dp - stats[1, at, here]) * scale
        return p.astype(BF16), ds.astype(BF16)

    steps = [(i, b) for i in range(groups) for b in range(rows // width)]
    ahead = scores(*steps[0])
    for m, (i, b) in enumerate(steps):
        now = ahead
        if m + 1 < len(steps):
            ahead = scores(*steps[m + 1])
        p, ds = weights(i, b, *now)
        qb, gb, keys, here = operands(i, b)
        accs[i][1, keys, :] += dot(p, gb, INNER)
        accs[i][0, keys, :] += dot(ds, qb, INNER)
        dq[i, here, :] = dot(ds, kcat[i, keys, :], DOWN).astype(BF16)
    if add:
        prev = refs[0]
        for n in range(2):
            for i in range(groups):
                prev[n, i] = accs[i][n, pl.ds(length, length), :].astype(BF16)


def attention(side, place, q, g, stats, kv, accs, spots, ours, scale):
    length, dim = kv[0].shape[2:]
    rows = stats.shape[2]
    groups = len(spots)
    add = accs is not None
    out_shape = [jax.ShapeDtypeStruct((groups, rows, dim), BF16)]
    out_shape += [jax.ShapeDtypeStruct((2, 3 * length, dim), F32)] * groups
    if add:
        out_shape += [jax.ShapeDtypeStruct((2, groups, length, dim), BF16)]
    operands = [q, g, stats, *kv] + list(accs or ())
    flops = 2 * 5 * groups * rows * (2 * length + 64) * dim
    return pl.pallas_call(
        functools.partial(attn_kernel, scale, spots, ours, add),
        in_specs=[SMEM, SMEM] + [VMEM] * len(operands),
        out_specs=[VMEM] * len(out_shape),
        out_shape=out_shape,
        scratch_shapes=[pltpu.VMEM((groups, 3 * length, dim), BF16)] * 2 + [pltpu.VMEM((2, rows, dim), BF16)] * 2,
        input_output_aliases={9 + i: 1 + i for i in range(groups)} if add else {},
        compiler_params=params(16),
        cost_estimate=pl.CostEstimate(flops=flops, bytes_accessed=0, transcendentals=0),
        name="attention",
    )(side, place, *operands)


def body(queries, keys, values, outputs, output_gradient, lse):
    _, heads_all, dim = queries.shape
    _, heads_kv, _ = keys.shape
    side = lax.axis_index("head")
    heads = heads_all // lax.axis_size("head")
    per = heads // heads_kv
    chunks = heads_kv // 2
    pair = 2 * per
    scale = dim ** (-0.5)
    side_s = side.astype(jnp.int32).reshape(1)
    place_s = lax.axis_index("seq").astype(jnp.int32).reshape(1)

    packed = [first(side_s, place_s, queries, heads, pair)]
    packed.append(first(side_s, place_s, output_gradient, heads, pair))
    own_kv, *chunk_kv = split(keys, values, chunks)
    far_kv, far_next = [], []
    for i in range(chunks):
        far_kv.append(turned(chunk_kv[i], "seq", 2))
        far_next.append(swapped(far_kv[i], "seq"))
    own_next = swapped(own_kv, "seq")
    stats, stats_other = row_stats(side_s, output_gradient, outputs, lse, per)
    stats_got = swapped(stats_other, "head")
    others = rest(side_s, queries, output_gradient, heads, pair)
    mine_rows = others[2 * (chunks - 1) :]
    got = []
    got.append([swapped(packed[0], "head")])
    got[0].append(swapped(packed[1], "head"))
    for i, two in enumerate(others[: 2 * (chunks - 1)]):
        got.append([swapped(two, "head")] * 2)

    run = functools.partial(attention, side_s, place_s, scale=scale)
    ours, theirs, accs, prev_got, back_got = [], [], [], [], []
    count = 0
    for i in range(chunks):
        kv = (far_kv[i], far_next[i], own_next, own_kv)
        spots = tuple((j, 2 * i + j, j) for j in range(2))
        dq, *acc = run(*mine_rows[2 * i : 2 * i + 2], stats, kv, None, spots, True)
        ours.append(dq)
        for task in ((0, 1),) if i == 0 else ((0,), (1,)):
            spots = tuple((j if i == 0 else 0, 2 * i + j, j) for j in task)
            dq, *out, prev = run(*got[count], stats_got, kv, [acc[j] for j in task], spots, False)
            accs += out
            prev_got.append(swapped(prev, "seq"))
            theirs.append(swapped(dq, "head"))
            back_got.append(turned(merge(place_s, out, prev_got[-1]), "seq", -2))
            count += 1
    plan = [((i, 0), (i, 1), True, i * pair) for i in range(chunks)]
    plan += [((chunks, 0), (chunks, 1), False, 0)]
    plan += [((chunks + 2 * i - 1, 0), (chunks + 2 * i, 0), False, i * pair) for i in range(1, chunks - 1)]
    whole = place(side_s, ours + theirs[:-2], tuple(plan), None, queries.shape, heads, pair)
    plan = (((0, 0), (1, 0), False, (chunks - 1) * pair),)
    whole = place(side_s, theirs[-2:], plan, whole, queries.shape, heads, pair)
    wide = gather(place_s, lax.axis_size("seq"), accs, prev_got, back_got[:-1])
    return whole, *join(place_s, lax.axis_size("seq"), back_got[-1], wide)


def solution(mesh):
    assert mesh.shape["head"] == 2

    return jax.shard_map(
        body,
        mesh=mesh,
        in_specs=(
            P(("seq", "head"), None, None),
            P("seq", "head", None),
            P("seq", "head", None),
            P(("seq", "head"), None, None),
            P(("seq", "head"), None, None),
            P(("seq", "head"), None),
        ),
        out_specs=(P(("seq", "head"), None, None), P("seq", "head", None), P("seq", "head", None)),
        check_vma=False,
    )
```

```python
import functools
import math

import jax
import jax.numpy as jnp
from jax import lax
from jax.experimental import pallas as pl
from jax.experimental.pallas import tpu as pltpu
from jax.sharding import PartitionSpec as P


LOG2E = math.log2(math.e)
F32 = jnp.float32
BF16 = jnp.bfloat16
ACROSS = ((1,), (1,))
INNER = ((1,), (0,))
DOWN = ((0,), (0,))
VMEM = pl.BlockSpec(memory_space=pltpu.VMEM)
SMEM = pl.BlockSpec(memory_space=pltpu.SMEM)
ANY = pl.BlockSpec(memory_space=pl.ANY)
HBM = pl.BlockSpec(memory_space=pltpu.HBM)


def turned(shard, axis, by):
    size = lax.axis_size(axis)
    return lax.ppermute(shard, axis, [(i, (i + by) % size) for i in range(size)])


def swapped(shard, axis):
    return lax.ppermute(shard, axis, [(i, i ^ 1) for i in range(lax.axis_size(axis))])


def dot(a, b, dims):
    return lax.dot_general(a, b, (dims, ((), ())), preferred_element_type=F32)


def params(mib):
    return pltpu.CompilerParams(vmem_limit_bytes=mib * 2**20)


def untangle(x):
    tokens, heads, dim = x.shape
    x = x.astype(F32).reshape(tokens // 2, 2, heads, dim)
    a, b = x[:, 0], x[:, 1]
    low = lax.broadcasted_iota(jnp.int32, a.shape, 1) < heads // 2
    first = jnp.where(low, a, pltpu.roll(b, heads // 2, axis=1))
    second = jnp.where(low, pltpu.roll(a, heads // 2, axis=1), b)
    return [y.reshape(-1, dim).astype(BF16) for y in (first, second)]


def tangle(first, second, tokens):
    rows, dim = first.shape
    heads = 2 * rows // tokens
    a, b = (y.astype(F32).reshape(tokens // 2, heads, dim) for y in (first, second))
    low = lax.broadcasted_iota(jnp.int32, a.shape, 1) < heads // 2
    even = jnp.where(low, a, pltpu.roll(b, heads // 2, axis=1))
    odd = jnp.where(low, pltpu.roll(a, heads // 2, axis=1), b)
    return jnp.stack([even, odd], 1).reshape(tokens, heads, dim).astype(BF16)


def first_kernel(heads, pair, side_ref, place_ref, src, out, sem):
    start = pl.multiple_of((1 - side_ref[0]) * heads, pair)
    parts = sem.shape[0]
    size = src.shape[0] // parts
    copies = []
    for m in range(parts):
        here = pl.ds(m * size, size)
        copies.append(pltpu.make_async_copy(src.at[here, pl.ds(start, pair), :], out.at[here], sem.at[m]))
        copies[-1].start()
    for copy in copies:
        copy.wait()


def first(side, place, x, heads, pair):
    tokens, _, dim = x.shape
    return pl.pallas_call(
        functools.partial(first_kernel, heads, pair),
        in_specs=[SMEM, SMEM, HBM],
        out_specs=VMEM,
        out_shape=jax.ShapeDtypeStruct((tokens, pair, dim), BF16),
        scratch_shapes=[pltpu.SemaphoreType.DMA((4,))],
        compiler_params=params(2),
        name="first",
    )(side, place, pltpu.with_memory_space_constraint(x, pltpu.HBM))


def rest_kernel(heads, pair, side_ref, q, g, *outs):
    outs = list(outs)
    count = heads // pair
    for i in range(1, count):
        start = pl.multiple_of((1 - side_ref[0]) * heads + i * pair, pair)
        rows = [untangle(src[:, pl.ds(start, pair), :]) for src in (q, g)]
        for j in range(2):
            out = outs.pop(0)
            for n in range(2):
                out[n] = rows[n][j]
    for i in range(count):
        start = pl.multiple_of(side_ref[0] * heads + i * pair, pair)
        for src in (q, g):
            out = outs.pop(0)
            out[0], out[1] = untangle(src[:, pl.ds(start, pair), :])


def rest(side, queries, gradient, heads, pair):
    tokens, _, dim = queries.shape
    count = heads // pair
    sizes = [2] * (2 * (count - 1)) + [2] * (2 * count)
    return pl.pallas_call(
        functools.partial(rest_kernel, heads, pair),
        in_specs=[SMEM, VMEM, VMEM],
        out_specs=[VMEM] * len(sizes),
        out_shape=[jax.ShapeDtypeStruct((n, tokens * pair // 2, dim), BF16) for n in sizes],
        compiler_params=params(4),
        name="rest",
    )(side, queries, gradient)


def split_kernel(k, v, whole, *refs):
    outs, (wide, buf, sem) = refs[:-3], refs[-3:]
    heads, length = whole.shape[1:3]
    groups = heads // len(outs)
    parts = sem.shape[1]
    size = k.shape[0] // parts
    copies = []
    for n, src in enumerate((k, v)):
        for m in range(parts):
            here = pl.ds(m * size, size)
            copies.append(pltpu.make_async_copy(src.at[here], buf.at[n, here], sem.at[n, m]))
            copies[-1].start()
    for n in range(2):
        for m in range(parts):
            copies[n * parts + m].wait()
        wide[...] = buf[n].astype(F32)
        for i in range(heads):
            x = wide[pl.ds(i, length, stride=heads), :].astype(BF16)
            whole[n, i] = x
            outs[i // groups][n, i % groups] = x


def split(keys, values, chunks):
    length, heads, dim = keys.shape
    sizes = [heads] + [heads // chunks] * chunks
    return pl.pallas_call(
        split_kernel,
        in_specs=[HBM, HBM],
        out_specs=[VMEM] * (1 + chunks),
        out_shape=[jax.ShapeDtypeStruct((2, n, length, dim), BF16) for n in sizes],
        scratch_shapes=[
            pltpu.VMEM((length * heads, dim), F32),
            pltpu.VMEM((2, length * heads, dim), BF16),
            pltpu.SemaphoreType.DMA((2, 2)),
        ],
        compiler_params=params(4),
        name="split",
    )(*(pltpu.with_memory_space_constraint(x.reshape(-1, dim), pltpu.HBM) for x in (keys, values)))


def parts_of(x, count):
    terms = []
    for _ in range(count):
        terms.append(x.astype(BF16))
        x = x - terms[-1].astype(F32)
    return terms


def stats_kernel(per, side_ref, g, o, lse, ours, other, rep, both):
    tokens, heads_all, dim = g.shape
    rows = tokens * per
    groups = heads_all // per
    lane = lax.broadcasted_iota(jnp.int32, (1, rows), 1)
    token = lax.broadcasted_iota(jnp.int32, (tokens, 1), 0)
    spread = (token == lane // per).astype(F32).astype(BF16)
    for n, term in enumerate(parts_of(lse[...] * LOG2E, 3)):
        part = dot(term, spread, INNER)
        if n == 0:
            rep[...] = part
        else:
            rep[...] += part
    for m in range(groups):
        line = rep[pl.ds(m * per, 1), :]
        for i in range(1, per):
            line = jnp.where(lane % per == i, rep[pl.ds(m * per + i, 1), :], line)
        both[0, pl.ds(m, 1), :] = line
    block = dim // per
    sub = lax.broadcasted_iota(jnp.int32, (1, 2 * per, dim), 1)
    cell = lax.broadcasted_iota(jnp.int32, (1, 2 * per, dim), 2)
    cell = jnp.where(cell % per == sub % per, cell // per, -1)
    which = lax.broadcasted_iota(jnp.int32, (block, 1, 1), 0)

    def tokens_block(t, carry):
        here = pl.ds(pl.multiple_of(t * block, block), block)
        line = pl.ds(pl.multiple_of(t * dim, dim), dim)
        for m in range(groups // 2):
            pick = pl.ds(2 * per * m, 2 * per)
            x = g[here, pick, :].astype(F32) * o[here, pick, :].astype(F32)
            x = jnp.sum(x, axis=-1, keepdims=True)
            x = jnp.sum(jnp.where(cell == which, x, 0.0), axis=0)
            for n in range(2):
                both[1, pl.ds(2 * m + n, 1), line] = jnp.sum(x[n * per : (n + 1) * per], axis=0, keepdims=True)
        return carry

    lax.fori_loop(0, tokens // block, tokens_block, 0)
    half = groups // 2
    side = side_ref[0]
    for n in range(2):
        low, high = both[n, pl.ds(0, half), :], both[n, pl.ds(half, half), :]
        ours[n] = jnp.where(side == 0, low, high)
        other[n] = jnp.where(side == 0, high, low)


def row_stats(side, gradient, outputs, lse, per):
    tokens, heads_all, _ = gradient.shape
    groups, rows = heads_all // per, tokens * per
    return pl.pallas_call(
        functools.partial(stats_kernel, per),
        in_specs=[SMEM, VMEM, VMEM, VMEM],
        out_specs=[VMEM, VMEM],
        out_shape=[jax.ShapeDtypeStruct((2, groups // 2, rows), F32)] * 2,
        scratch_shapes=[pltpu.VMEM((heads_all, rows), F32), pltpu.VMEM((2, groups, rows), F32)],
        compiler_params=params(8),
        name="row_stats",
    )(side, gradient, outputs, lse.T)


def gather_kernel(where, blocks, place_ref, *refs):
    groups = len(where)
    here, came, outs = refs[:groups], refs[groups:-2], refs[-2:]
    prev, back = came[: len(came) // 2 + 1], came[len(came) // 2 + 1 :]
    length = outs[0].shape[0] // groups
    even = place_ref[0] % 2 == 0
    inside = place_ref[0] < blocks - 2
    for n, out in enumerate(outs):
        for i, (m, at) in enumerate(where):
            total = here[i][n, pl.ds(2 * length, length), :]
            total += jnp.where(even, prev[m][n, at].astype(F32), 0.0)
            if m < len(back):
                total += jnp.where(inside, back[m][n, at].astype(F32), 0.0)
            out[pl.ds(i, length, stride=groups), :] = total


def gather(place, blocks, here, prev, back):
    groups = len(here)
    where = tuple((m, at) for m, x in enumerate(prev) for at in range(x.shape[1]))
    length, dim = prev[0].shape[2:]
    return pl.pallas_call(
        functools.partial(gather_kernel, where, blocks),
        in_specs=[SMEM] + [VMEM] * (groups + len(prev) + len(back)),
        out_specs=[VMEM] * 2,
        out_shape=[jax.ShapeDtypeStruct((length * groups, dim), F32)] * 2,
        compiler_params=params(2),
        name="gather",
    )(place, *here, *prev, *back)


def join_kernel(blocks, place_ref, last, wide_k, wide_v, out_k, out_v, sum_k, sum_v):
    length = last.shape[2]
    groups = wide_k.shape[0] // length
    inside = place_ref[0] < blocks - 2
    for n, (out, total) in enumerate(((out_k, sum_k), (out_v, sum_v))):
        rows = pl.ds(groups - 1, length, stride=groups)
        total[rows, :] = total[rows, :] + jnp.where(inside, last[n, 0].astype(F32), 0.0)
        out[...] = total[...].astype(BF16)


def join(place, blocks, last, wide):
    shape = wide[0].shape
    length, dim = last.shape[2:]
    outs = pl.pallas_call(
        functools.partial(join_kernel, blocks),
        in_specs=[SMEM] + [VMEM] * 3,
        out_specs=[VMEM] * 4,
        out_shape=[jax.ShapeDtypeStruct(shape, t) for t in (BF16, BF16, F32, F32)],
        input_output_aliases={2: 2, 3: 3},
        compiler_params=params(2),
        name="join",
    )(place, last, *wide)
    return [x.reshape(length, shape[0] // length, dim) for x in outs[:2]]


def merge_kernel(place_ref, *refs):
    here, prev, out = refs[:-2], refs[-2], refs[-1]
    length = prev.shape[2]
    odd = place_ref[0] % 2 == 1
    for n in range(2):
        for i, acc in enumerate(here):
            out[n, i] = (acc[n, pl.ds(0, length), :] + jnp.where(odd, prev[n, i].astype(F32), 0.0)).astype(BF16)


def merge(place, here, prev):
    return pl.pallas_call(
        merge_kernel,
        in_specs=[SMEM] + [VMEM] * (len(here) + 1),
        out_specs=VMEM,
        out_shape=jax.ShapeDtypeStruct(prev.shape, BF16),
        compiler_params=params(2),
        name="merge",
    )(place, *here, prev)


def place_kernel(plan, heads, side_ref, *refs):
    buf, sem = refs[-2:]
    out = refs[-3]
    tokens, pair = buf.shape[1:3]
    copies = []
    for m, (a, b, ours, first) in enumerate(plan):
        side = side_ref[0] if ours else 1 - side_ref[0]
        start = pl.multiple_of(side * heads + first, pair)
        rows = refs[a[0]].shape[1]
        parts = sem.shape[1]
        for j in range(parts):
            some = pl.ds(j * (rows // parts), rows // parts)
            here = pl.ds(j * (tokens // parts), tokens // parts)
            buf[m, here] = tangle(refs[a[0]][a[1], some, :], refs[b[0]][b[1], some, :], tokens // parts)
            view = out.at[here, pl.ds(start, pair), :]
            copies.append(pltpu.make_async_copy(buf.at[m, here], view, sem.at[m, j]))
            copies[-1].start()
    for copy in copies:
        copy.wait()


def place(side, pieces, plan, whole, shape, heads, pair):
    more = [] if whole is None else [whole]
    return pl.pallas_call(
        functools.partial(place_kernel, plan, heads),
        in_specs=[SMEM] + [VMEM] * len(pieces) + [ANY] * len(more),
        out_specs=ANY,
        out_shape=jax.ShapeDtypeStruct(shape, BF16),
        scratch_shapes=[
            pltpu.VMEM((len(plan), shape[0], pair, shape[2]), BF16),
            pltpu.SemaphoreType.DMA((len(plan), 4)),
        ],
        input_output_aliases={1 + len(pieces): 0} if more else {},
        compiler_params=params(4),
        name="place",
    )(side, *pieces, *more)


def attn_kernel(scale, spots, ours, add, side_ref, place_ref, q, g, stats, far, far_next, own_next, own, *refs):
    groups = len(spots)
    refs = list(refs[groups:] if add else refs)
    dq = refs.pop(0)
    accs = [refs.pop(0) for _ in range(groups)]
    kcat, vcat, qs, gs = refs[-4:]
    length = own.shape[2]
    rows, dim = dq.shape[1:]
    behind = 0 if ours else 1
    if q.shape[1] != rows:
        behind = 0
        for src, dst in ((q, qs), (g, gs)):
            dst[0], dst[1] = untangle(src[...])
        q, g = qs, gs
    place = place_ref[0]

    def fill(block, src, index, when):
        here = pl.ds(block * length, length)

        @pl.when(when)
        def _():
            for i, spot in enumerate(spots):
                kcat[i, here, :] = jnp.zeros((length, dim), BF16) if src is None else src[0, spot[index]]
                vcat[i, here, :] = jnp.zeros((length, dim), BF16) if src is None else src[1, spot[index]]

    fill(0, far, 2, place >= 2)
    fill(0, None, 2, place < 2)
    fill(1, own_next, 1, place % 2 == 1)
    fill(1, far_next, 2, jnp.logical_and(place % 2 == 0, place >= 2))
    fill(1, None, 2, place < 1)
    fill(2, own, 1, place >= 0)
    if not add:
        for acc in accs:
            acc[...] = jnp.zeros_like(acc)

    width = 256
    half = length // 2
    per = rows // half
    span = width // per
    window = 2 * length
    token = lax.broadcasted_iota(jnp.int32, (1, width), 1) // per
    key_id = lax.broadcasted_iota(jnp.int32, (span, 1), 0)
    side = side_ref[0] if ours else 1 - side_ref[0]
    off = pl.multiple_of(side * half, span)

    def operands(i, b):
        here = pl.ds(b * width, width)
        keys = pl.ds(pl.multiple_of(off + b * span, span), window + span)
        return q[spots[i][0], here, :], g[spots[i][0] + behind, here, :], keys, here

    def scores(i, b):
        qb, gb, keys, _ = operands(i, b)
        return dot(kcat[i, keys, :], qb, ACROSS), dot(vcat[i, keys, :], gb, ACROSS)

    def weights(i, b, s, dp):
        here = pl.ds(b * width, width)
        at = pl.ds(spots[i][1], 1)
        p = jnp.exp2(s * (scale * LOG2E) - stats[0, at, here])
        first = jnp.where(key_id > token, p[:span], 0.0)
        last = jnp.where(key_id <= token, p[window:], 0.0)
        p = jnp.concatenate([first, p[span:window], last], 0)
        ds = p * (dp - stats[1, at, here]) * scale
        return p.astype(BF16), ds.astype(BF16)

    steps = [(i, b) for i in range(groups) for b in range(rows // width)]
    ahead = scores(*steps[0])
    for m, (i, b) in enumerate(steps):
        now = ahead
        if m + 1 < len(steps):
            ahead = scores(*steps[m + 1])
        p, ds = weights(i, b, *now)
        qb, gb, keys, here = operands(i, b)
        accs[i][1, keys, :] += dot(p, gb, INNER)
        accs[i][0, keys, :] += dot(ds, qb, INNER)
        dq[i, here, :] = dot(ds, kcat[i, keys, :], DOWN).astype(BF16)
    if add:
        prev = refs[0]
        for n in range(2):
            for i in range(groups):
                prev[n, i] = accs[i][n, pl.ds(length, length), :].astype(BF16)


def attention(side, place, q, g, stats, kv, accs, spots, ours, scale):
    length, dim = kv[0].shape[2:]
    rows = stats.shape[2]
    groups = len(spots)
    add = accs is not None
    out_shape = [jax.ShapeDtypeStruct((groups, rows, dim), BF16)]
    out_shape += [jax.ShapeDtypeStruct((2, 3 * length, dim), F32)] * groups
    if add:
        out_shape += [jax.ShapeDtypeStruct((2, groups, length, dim), BF16)]
    operands = [q, g, stats, *kv] + list(accs or ())
    flops = 2 * 5 * groups * rows * (2 * length + 64) * dim
    return pl.pallas_call(
        functools.partial(attn_kernel, scale, spots, ours, add),
        in_specs=[SMEM, SMEM] + [VMEM] * len(operands),
        out_specs=[VMEM] * len(out_shape),
        out_shape=out_shape,
        scratch_shapes=[pltpu.VMEM((groups, 3 * length, dim), BF16)] * 2 + [pltpu.VMEM((2, rows, dim), BF16)] * 2,
        input_output_aliases={9 + i: 1 + i for i in range(groups)} if add else {},
        compiler_params=params(16),
        cost_estimate=pl.CostEstimate(flops=flops, bytes_accessed=0, transcendentals=0),
        name="attention",
    )(side, place, *operands)


def body(queries, keys, values, outputs, output_gradient, lse):
    _, heads_all, dim = queries.shape
    _, heads_kv, _ = keys.shape
    side = lax.axis_index("head")
    heads = heads_all // lax.axis_size("head")
    per = heads // heads_kv
    chunks = heads_kv // 2
    pair = 2 * per
    scale = dim ** (-0.5)
    side_s = side.astype(jnp.int32).reshape(1)
    place_s = lax.axis_index("seq").astype(jnp.int32).reshape(1)

    packed = [first(side_s, place_s, queries, heads, pair)]
    packed.append(first(side_s, place_s, output_gradient, heads, pair))
    own_kv, *chunk_kv = split(keys, values, chunks)
    far_kv, far_next = [], []
    for i in range(chunks):
        far_kv.append(turned(chunk_kv[i], "seq", 2))
        far_next.append(swapped(far_kv[i], "seq"))
    own_next = swapped(own_kv, "seq")
    stats, stats_other = row_stats(side_s, output_gradient, outputs, lse, per)
    stats_got = swapped(stats_other, "head")
    others = rest(side_s, queries, output_gradient, heads, pair)
    mine_rows = others[2 * (chunks - 1) :]
    got = []
    got.append([swapped(packed[0], "head")])
    got[0].append(swapped(packed[1], "head"))
    for i, two in enumerate(others[: 2 * (chunks - 1)]):
        got.append([swapped(two, "head")] * 2)

    run = functools.partial(attention, side_s, place_s, scale=scale)
    ours, theirs, accs, prev_got, back_got = [], [], [], [], []
    count = 0
    for i in range(chunks):
        kv = (far_kv[i], far_next[i], own_next, own_kv)
        spots = tuple((j, 2 * i + j, j) for j in range(2))
        dq, *acc = run(*mine_rows[2 * i : 2 * i + 2], stats, kv, None, spots, True)
        ours.append(dq)
        for task in ((0, 1),) if i == 0 else ((0,), (1,)):
            spots = tuple((j if i == 0 else 0, 2 * i + j, j) for j in task)
            dq, *out, prev = run(*got[count], stats_got, kv, [acc[j] for j in task], spots, False)
            accs += out
            prev_got.append(swapped(prev, "seq"))
            theirs.append(swapped(dq, "head"))
            back_got.append(turned(merge(place_s, out, prev_got[-1]), "seq", -2))
            count += 1
    plan = [((i, 0), (i, 1), True, i * pair) for i in range(chunks)]
    plan += [((chunks, 0), (chunks, 1), False, 0)]
    plan += [((chunks + 2 * i - 1, 0), (chunks + 2 * i, 0), False, i * pair) for i in range(1, chunks - 1)]
    whole = place(side_s, ours + theirs[:-2], tuple(plan), None, queries.shape, heads, pair)
    plan = (((0, 0), (1, 0), False, (chunks - 1) * pair),)
    whole = place(side_s, theirs[-2:], plan, whole, queries.shape, heads, pair)
    wide = gather(place_s, lax.axis_size("seq"), accs, prev_got, back_got[:-1])
    return whole, *join(place_s, lax.axis_size("seq"), back_got[-1], wide)


def solution(mesh):
    assert mesh.shape["head"] == 2

    return jax.shard_map(
        body,
        mesh=mesh,
        in_specs=(
            P(("seq", "head"), None, None),
            P("seq", "head", None),
            P("seq", "head", None),
            P(("seq", "head"), None, None),
            P(("seq", "head"), None, None),
            P(("seq", "head"), None),
        ),
        out_specs=(P(("seq", "head"), None, None), P("seq", "head", None), P("seq", "head", None)),
        check_vma=False,
    )
```
